32 devices in a mesh: job: 2 (over x), samp: 8 (over z, y), tok: 2 (over core).
Axes of the slice: x: 2, y: 2, z: 4, core: 2. Of those that a mesh axis runs over, the one named last changes fastest.
Arguments:
- acts: bfloat16 [16, 384, 768], P(('job', 'samp'), 'tok'), parts along dimension 0, may hold values from -6 to 6
- out_grad: bfloat16 [16, 384, 768], P(('job', 'samp'), 'tok'), parts along dimension 0, may hold values from -6 to 6
- pair: bfloat16 [768, 384, 128], P(('job', 'tok'), 'samp'), parts along dimension 0, may hold values from -1000 to 1000
- chain_of_token: int32 [768], P('job'), parts along dimension 0, may hold values from 0 to 7, never falling along the last dimension, each value on 1 to 96 neighbouring positions
- w_query: bfloat16 [768, 768], replicated, may hold values from -0.21875 to 0.21875
- w_key: bfloat16 [768, 768], replicated, may hold values from -0.21875 to 0.21875
- w_value: bfloat16 [768, 768], replicated, may hold values from -0.21875 to 0.21875
- w_out: bfloat16 [768, 768], replicated, may hold values from -0.21875 to 0.21875
- w_pair: bfloat16 [128, 16], replicated, may hold values from -0.5 to 0.5
Outputs:
- act_grad: bfloat16 [16, 384, 768], P(('job', 'samp'), 'tok'), parts along dimension 0
- pair_grad: float32 [768, 384, 128], P(('job', 'tok'), 'samp'), parts along dimension 0
- weight_grads: float32 [6144, 768], P(('job', 'samp', 'tok')), parts along dimension 0
- pair_weight_grad: float32 [256, 16], P('job'), parts along dimension 0
The draws below stay inside these ranges and needn't reach their ends.
There are 2 independent parts, one for each index of `job`. The reference program is written for one: setup_inputs(seed, part) draws one part's arguments, and reference() takes and returns one part's arrays. A program takes and returns all parts, laid end to end along the dimension named above; an argument that names none is the same for every part. Nothing has to cross between parts.
All inputs are finite; a program needn't handle non-finite values.
Results may differ from the reference program's by a relative error of at most 0.03.
The reference program's roundings to bfloat16 on the way (of `pair_bias`, `probs_low`, `mixed`, `upstream` and `query_grad`) count: a program that leaves them out, or rounds other values in their place, can miss the bound.
Values may be sent and summed in bfloat16 or wider, within the bound.
A program may use at most 64 MiB of HBM per device.

```python
import math
import jax
import jax.numpy as jnp
import numpy as np
from jax import lax

D = 768
H = 16
CP = 128
HD = 48
CHAINS = 8
SAMPLES = 8
NTOK = 384


def draw_pair(key, part):
    key_base = jax.random.fold_in(jax.random.fold_in(key, 11), 0)
    base = jnp.clip(jax.random.normal(key_base, (NTOK, NTOK, CP), jnp.float32), -6.0, 6.0)
    return base.astype(jnp.bfloat16)


def spiked(result, stream_key, source, target, shards_of, factor):
    def block_of(axis_at):
        return (jnp.arange(result.shape[axis_at]) // (result.shape[axis_at] // shards_of)).reshape((-1,) + (1,) * (result.ndim - 1 - axis_at))

    first = jax.random.permutation(stream_key, shards_of)[block_of(target)]
    far = (block_of(target) + shards_of // 2) % shards_of
    return jnp.where((block_of(source) == first) | (block_of(source) == far), factor * result, result)


def shard_levels(stream_key, shape, pieces, smallest, high):
    gain = 1.0
    for position, blocks in pieces:
        heights = jax.random.uniform(jax.random.fold_in(jax.random.fold_in(stream_key, 6), position), (blocks,), jnp.float32, smallest / len(pieces), high / len(pieces))
        gain = gain * jnp.repeat(jnp.exp(heights), shape[position] // blocks).reshape((-1,) + (1,) * (len(shape) - 1 - position))
    return gain


def profile(count, total, bound, slope):
    weights = [(1 << 20) // math.isqrt(standing ** slope) + 1 for standing in range(2, count + 1)]
    rest, holding = total - bound - (count - 1), [1] * (count - 1)
    while rest > 0:
        movable = [i for i in range(count - 1) if holding[i] < bound]
        whole, left = sum([weights[i] for i in movable]), rest
        for i in movable:
            extra = min(bound - holding[i], max(1, left * weights[i] // whole), rest)
            holding[i] = holding[i] + extra
            rest = rest - extra
    return np.array([bound] + holding)


def uneven(key, count, total, reach, slope):
    if count == 2:
        one = jax.random.randint(key, (), max(1, total - reach), min(reach, total - 1) + 1)
        return jnp.stack([one, total - one])
    sizes = jnp.asarray(profile(count, total, reach, slope), jnp.int32)
    twos = (count - 1) // 2
    donor, sink = sizes[1:1 + 2 * twos:2], sizes[2:2 + 2 * twos:2]
    margin = jnp.minimum(donor - 1, reach - sink)
    passed = jax.random.randint(jax.random.fold_in(key, 1), (twos,), 0, 1 << 20) % (margin + 1)
    sizes = sizes.at[1:1 + 2 * twos:2].set(donor - passed).at[2:2 + 2 * twos:2].set(sink + passed)
    return sizes[jax.random.permutation(jax.random.fold_in(key, 2), count)]


def scatter_about(rng, extent, spread, bound, cuts=(), dtype=jnp.bfloat16):
    array = spread * jax.random.normal(rng, extent, jnp.float32)
    if cuts:
        array = array * shard_levels(rng, extent, cuts, -0.22, 0.18)
    return jnp.clip(array, -bound, bound).astype(dtype)


def gaussian_with(rng, dims, scale, bound, shards, heavy, dtype=jnp.bfloat16):
    result = scale * jax.random.normal(rng, dims, jnp.float32)
    if shards:
        result = result * shard_levels(rng, dims, shards, -0.22, 0.18)
    return jnp.clip(spiked(result, jax.random.fold_in(rng, 3), *heavy), -bound, bound).astype(dtype)


def setup_inputs(seed: int = 0, part: int = 0) -> dict:
    seeds = jax.random.split(jax.random.key(seed), 10)
    own_keys = jax.random.split(jax.random.fold_in(seeds[9], part), 10)
    acts = gaussian_with(own_keys[0], (SAMPLES, NTOK, D), 1.0, 6.0, ((0, 8), (1, 2)), (0, 2, 8, 2.0))
    out_grad = scatter_about(own_keys[1], (SAMPLES, NTOK, D), 1.0, 6.0, ((0, 8), (1, 2)))
    pair = draw_pair(jax.random.fold_in(jax.random.fold_in(seeds[9], part), 71), part)
    chain_of_token = jnp.searchsorted(jnp.cumsum(uneven(own_keys[3], CHAINS, NTOK, NTOK // 4, 0)), jnp.arange(NTOK), side="right").astype(jnp.int32)
    w_query = scatter_about(seeds[4], (D, D), D ** -0.5, 0.21875)
    w_key = scatter_about(seeds[5], (D, D), D ** -0.5, 0.21875)
    w_value = scatter_about(seeds[6], (D, D), D ** -0.5, 0.21875)
    w_out = scatter_about(seeds[7], (D, D), D ** -0.5, 0.21875)
    w_pair = scatter_about(seeds[8], (CP, H), CP ** -0.5, 0.5)
    return {"acts": acts, "out_grad": out_grad, "pair": pair, "chain_of_token": chain_of_token, "w_query": w_query, "w_key": w_key, "w_value": w_value, "w_out": w_out, "w_pair": w_pair}


CHAIN_REWARD = 2.0

def rounded(value):
    return lax.optimization_barrier(value.astype(jnp.bfloat16))

def reference(acts, out_grad, pair, chain_of_token, w_query, w_key, w_value, w_out, w_pair):
    score_scale = 1.0 / math.sqrt(HD)
    pair_bias = rounded(jnp.einsum('ijc,ch->hij', pair.astype(jnp.float32), w_pair.astype(jnp.float32), precision=lax.Precision.HIGHEST))
    matching_chain = (chain_of_token[:, None] == chain_of_token[None, :]).astype(jnp.float32) * CHAIN_REWARD
    logit_base = pair_bias.astype(jnp.float32) + matching_chain[None]

    def one_sample(carry, item):
        gradient_total, bias_sum = carry
        tokens, cotangent = item
        query = rounded(jnp.dot(tokens, w_query, preferred_element_type=jnp.float32)).reshape(NTOK, H, HD).astype(jnp.float32)
        key_rows = rounded(jnp.dot(tokens, w_key, preferred_element_type=jnp.float32)).reshape(NTOK, H, HD).astype(jnp.float32)
        value_rows = rounded(jnp.dot(tokens, w_value, preferred_element_type=jnp.float32)).reshape(NTOK, H, HD).astype(jnp.float32)
        scores = jnp.einsum('ihd,jhd->hij', query, key_rows) * score_scale + logit_base
        peak = lax.optimization_barrier(jnp.max(scores, axis=2, keepdims=True))
        exp_terms = jnp.exp(scores - peak)
        probs = exp_terms / lax.optimization_barrier(jnp.sum(exp_terms, axis=2, keepdims=True))
        probs_low = rounded(probs).astype(jnp.float32)
        mixed = rounded(jnp.einsum('hij,jhd->ihd', probs_low, value_rows)).reshape(NTOK, D)
        upstream = rounded(jnp.dot(cotangent, w_out.T, preferred_element_type=jnp.float32)).reshape(NTOK, H, HD).astype(jnp.float32)
        prob_grad = jnp.einsum('ihd,jhd->hij', upstream, value_rows)
        value_grad = rounded(jnp.einsum('hij,ihd->jhd', probs_low, upstream)).reshape(NTOK, D)
        middle_point = lax.optimization_barrier(jnp.sum(probs * prob_grad, axis=2, keepdims=True))
        score_grad = probs * (prob_grad - middle_point)
        score_low = rounded(score_grad).astype(jnp.float32)
        query_grad = rounded(jnp.einsum('hij,jhd->ihd', score_low, key_rows) * score_scale).reshape(NTOK, D)
        key_grad = rounded(jnp.einsum('hij,ihd->jhd', score_low, query) * score_scale).reshape(NTOK, D)
        act_grad = jnp.dot(query_grad, w_query.T, preferred_element_type=jnp.float32)
        act_grad = act_grad + jnp.dot(key_grad, w_key.T, preferred_element_type=jnp.float32)
        act_grad = act_grad + jnp.dot(value_grad, w_value.T, preferred_element_type=jnp.float32)
        stacked = jnp.concatenate([jnp.dot(tokens.T, query_grad, preferred_element_type=jnp.float32), jnp.dot(tokens.T, key_grad, preferred_element_type=jnp.float32), jnp.dot(tokens.T, value_grad, preferred_element_type=jnp.float32), jnp.dot(mixed.T, cotangent, preferred_element_type=jnp.float32)], 0)
        return ((gradient_total + stacked, bias_sum + score_grad), act_grad.astype(jnp.bfloat16))
    start_carry = (jnp.zeros((4 * D, D), jnp.float32), jnp.zeros((H, NTOK, NTOK), jnp.float32))
    (weight_grads, bias_grad), act_grad = lax.scan(one_sample, start_carry, (acts, out_grad))
    pair_grad = jnp.einsum('hij,ch->ijc', bias_grad, w_pair.astype(jnp.float32), precision=lax.Precision.HIGHEST)
    pair_weight_grad = jnp.einsum('ijc,hij->ch', pair.astype(jnp.float32), bias_grad, precision=lax.Precision.HIGHEST)
    return (act_grad, pair_grad, weight_grads, pair_weight_grad)
```

```python
import functools
import math

import jax
import jax.numpy as jnp
from jax import lax
from jax.experimental import pallas as pl
from jax.experimental.pallas import tpu as pltpu
from jax.sharding import PartitionSpec as P

CHAIN_REWARD = 2.0
MESH_ID = pl.DeviceIdType.MESH
F32 = jnp.float32
BF16 = jnp.bfloat16
VMEM_SPEC = pl.BlockSpec(memory_space=pltpu.VMEM)


def grid_place(samp_count):
    cols = 2 if samp_count % 2 == 0 else 1
    return samp_count // cols, cols


def at_samp(z, y, cols):
    return {"samp": z * cols + y}


def greet_line(rows, cols, z, y, extra=()):
    barrier = pltpu.get_barrier_semaphore()

    @pl.when(z > 0)
    def _():
        pl.semaphore_signal(barrier, 1, device_id=at_samp(z - 1, y, cols), device_id_type=MESH_ID)

    @pl.when(z < rows - 1)
    def _():
        pl.semaphore_signal(barrier, 1, device_id=at_samp(z + 1, y, cols), device_id_type=MESH_ID)

    others = list(extra)
    if cols == 2:
        others.append(at_samp(z, 1 - y, cols))
    for other in others:
        pl.semaphore_signal(barrier, 1, device_id=other, device_id_type=MESH_ID)
    count = len(others) + (z > 0).astype(jnp.int32) + (z < rows - 1).astype(jnp.int32)
    pl.semaphore_wait(barrier, count)


def gather_kernel(rows, cols, x_ref, out_ref, right_send, right_recv, left_send, left_recv,
                  side_send, side_recv):
    me = lax.axis_index("samp")
    z, y = me // cols, me % cols
    greet_line(rows, cols, z, y)

    def right(step):
        block = z - step
        return pltpu.make_async_remote_copy(
            src_ref=x_ref if step == 0 else out_ref.at[block * cols + y],
            dst_ref=out_ref.at[block * cols + y],
            send_sem=right_send.at[step], recv_sem=right_recv.at[step],
            device_id=at_samp(z + 1, y, cols), device_id_type=MESH_ID)

    def left(step):
        block = z + step
        return pltpu.make_async_remote_copy(
            src_ref=x_ref if step == 0 else out_ref.at[block * cols + y],
            dst_ref=out_ref.at[block * cols + y],
            send_sem=left_send.at[step], recv_sem=left_recv.at[step],
            device_id=at_samp(z - 1, y, cols), device_id_type=MESH_ID)

    def side(slot, block, own):
        return pltpu.make_async_remote_copy(
            src_ref=x_ref if own else out_ref.at[block * cols + y],
            dst_ref=out_ref.at[block * cols + y],
            send_sem=side_send.at[slot], recv_sem=side_recv.at[block],
            device_id=at_samp(z, 1 - y, cols), device_id_type=MESH_ID)

    def landed(block_index, sem):
        pltpu.make_async_copy(out_ref.at[block_index], out_ref.at[block_index], sem).wait()

    pl.when(z < rows - 1)(lambda: right(0).start())
    pl.when(z > 0)(lambda: left(0).start())
    if cols == 2:
        side(0, z, True).start()
    out_ref[me] = x_ref[...]
    for step in range(1, rows):
        @pl.when(z - step >= 0)
        def _():
            landed((z - step) * cols + y, right_recv.at[step - 1])

            @pl.when(z < rows - 1)
            def _():
                right(step).start()
            if cols == 2:
                side(2 * step - 1, z - step, False).start()

        @pl.when(z + step <= rows - 1)
        def _():
            landed((z + step) * cols + y, left_recv.at[step - 1])

            @pl.when(z > 0)
            def _():
                left(step).start()
            if cols == 2:
                side(2 * step, z + step, False).start()

    for step in range(rows):
        pl.when((z - step >= 0) & (z < rows - 1))(lambda: right(step).wait_send())
        pl.when((z + step <= rows - 1) & (z > 0))(lambda: left(step).wait_send())
        if cols == 2:
            if step == 0:
                side(0, z, True).wait_send()
            else:
                pl.when(z - step >= 0)(lambda: side(2 * step - 1, z - step, False).wait_send())
                pl.when(z + step <= rows - 1)(lambda: side(2 * step, z + step, False).wait_send())
    if cols == 2:
        for block in range(rows):
            landed(block * cols + 1 - y, side_recv.at[block])


def gather_over_samp(x, samp_count):
    rows, cols = grid_place(samp_count)
    dma = pltpu.SemaphoreType.DMA
    return pl.pallas_call(
        functools.partial(gather_kernel, rows, cols),
        out_shape=jax.ShapeDtypeStruct((samp_count,) + x.shape, x.dtype),
        in_specs=[VMEM_SPEC],
        out_specs=VMEM_SPEC,
        scratch_shapes=[dma((rows,)), dma((rows,)), dma((rows,)), dma((rows,)),
                        dma((2 * rows,)), dma((rows,))],
        compiler_params=pltpu.CompilerParams(
            collective_id=0, has_side_effects=True, vmem_limit_bytes=48 << 20),
        name="bias_gather",
    )(x)


def chunk_order(rows):
    order = []
    for k in range((rows + 1) // 2):
        order.append(rows - 1 - k)
        if k != rows - 1 - k:
            order.append(k)
    return order


def scatter_kernel(rows, cols, toks, small, *refs):
    refs = list(refs)
    x_ref = refs.pop(0)
    small_ref = refs.pop(0) if small else None
    out_ref = refs.pop(0)
    small_out = refs.pop(0) if small else None
    (core_recv, side_buf, side_recv, total, line_buf, right_buf, left_buf,
     core_ss, core_rs, side_ss, side_rs, line_ss, right_rs, left_rs) = refs[:14]
    me = lax.axis_index("samp")
    z, y = me // cols, me % cols
    t = lax.axis_index("tok") if toks == 2 else 0
    samp_count = rows * cols
    if small:
        all_buf, all_ss, all_rs = refs[14:]
        flat = me * toks + t
        everyone = samp_count * toks
        barrier = pltpu.get_barrier_semaphore()
        peers = []
        for step in range(1, everyone):
            peer = lax.rem(flat + step, everyone)
            peers.append({"samp": peer // toks, "tok": peer % toks})
        for peer in peers:
            pl.semaphore_signal(barrier, 1, device_id=peer, device_id_type=MESH_ID)
        pl.semaphore_wait(barrier, everyone - 1)
        small_copies = [
            pltpu.make_async_remote_copy(
                src_ref=small_ref, dst_ref=all_buf.at[k], send_sem=all_ss.at[k],
                recv_sem=all_rs.at[k], device_id=peer, device_id_type=MESH_ID)
            for k, peer in enumerate(peers)]
    else:
        greet_line(rows, cols, z, y)
        small_copies = []

    order = chunk_order(rows)

    def core_copy(index):
        return pltpu.make_async_remote_copy(
            src_ref=x_ref.at[index, 1 - t], dst_ref=core_recv.at[index],
            send_sem=core_ss.at[index], recv_sem=core_rs.at[index],
            device_id={"tok": 1 - t}, device_id_type=MESH_ID)

    def side_copy(d):
        return pltpu.make_async_remote_copy(
            src_ref=side_buf.at[d], dst_ref=side_recv.at[d],
            send_sem=side_ss.at[d], recv_sem=side_rs.at[d],
            device_id=at_samp(z, 1 - y, cols), device_id_type=MESH_ID)

    def right_copy(d):
        return pltpu.make_async_remote_copy(
            src_ref=line_buf.at[d], dst_ref=right_buf.at[d],
            send_sem=line_ss.at[d], recv_sem=right_rs.at[d],
            device_id=at_samp(z + 1, y, cols), device_id_type=MESH_ID)

    def left_copy(d):
        return pltpu.make_async_remote_copy(
            src_ref=line_buf.at[d], dst_ref=left_buf.at[d],
            send_sem=line_ss.at[d], recv_sem=left_rs.at[d],
            device_id=at_samp(z - 1, y, cols), device_id_type=MESH_ID)

    if toks == 2:
        for d in order:
            if cols == 2:
                core_copy(d * cols + 1 - y).start()
        for d in order:
            core_copy(d * cols + y).start()
    for copy in small_copies:
        copy.start()

    def local_sum(index):
        value = x_ref[index, t].astype(F32)
        if toks == 2:
            core_copy(index).wait_recv()
            value = value + core_recv[index].astype(F32)
        return value

    if cols == 2:
        for d in order:
            if toks == 2:
                side_buf[d] = local_sum(d * cols + 1 - y).astype(BF16)
            else:
                side_buf[d] = x_ref[d * cols + 1 - y, 0]
            side_copy(d).start()
    for d in order:
        value = local_sum(d * cols + y)
        if cols == 2:
            side_copy(d).wait_recv()
            value = value + side_recv[d].astype(F32)
        total[...] = value

        @pl.when(z < d)
        def _():
            @pl.when(z > 0)
            def _():
                right_copy(d).wait_recv()
                line_buf[d] = (total[...] + right_buf[d].astype(F32)).astype(BF16)

            @pl.when(z == 0)
            def _():
                line_buf[d] = total[...].astype(BF16)
            right_copy(d).start()

        @pl.when(z > d)
        def _():
            @pl.when(z < rows - 1)
            def _():
                left_copy(d).wait_recv()
                line_buf[d] = (total[...] + left_buf[d].astype(F32)).astype(BF16)

            @pl.when(z == rows - 1)
            def _():
                line_buf[d] = total[...].astype(BF16)
            left_copy(d).start()

        @pl.when(z == d)
        def _():
            out_ref[...] = total[...]

    @pl.when(z > 0)
    def _():
        right_copy(z).wait_recv()
        out_ref[...] += right_buf[z].astype(F32)

    @pl.when(z < rows - 1)
    def _():
        left_copy(z).wait_recv()
        out_ref[...] += left_buf[z].astype(F32)

    if small:
        whole = small_ref[...]
        for k, copy in enumerate(small_copies):
            copy.wait_recv()
            whole = whole + all_buf[k]
        small_out[...] = whole
    for copy in small_copies:
        copy.wait_send()
    for d in range(rows):
        pl.when(z < d)(lambda: right_copy(d).wait_send())
        pl.when(z > d)(lambda: left_copy(d).wait_send())
        if cols == 2:
            side_copy(d).wait_send()
        if toks == 2:
            for c in range(cols):
                core_copy(d * cols + c).wait_send()


def scatter_over_samp(x, collective_id, small=None):
    samp_count, toks = x.shape[:2]
    chunk = x.shape[2:]
    rows, cols = grid_place(samp_count)
    dma = pltpu.SemaphoreType.DMA
    line = pltpu.VMEM((rows,) + chunk, BF16)
    scratch = [
        pltpu.VMEM(((samp_count if toks == 2 else 1),) + chunk, BF16),
        line, line, pltpu.VMEM(chunk, F32), line, line, line,
        dma((samp_count,)), dma((samp_count,)), dma((rows,)), dma((rows,)),
        dma((rows,)), dma((rows,)), dma((rows,))]
    out_shape = [jax.ShapeDtypeStruct(chunk, F32)]
    operands = [x]
    if small is not None:
        everyone = samp_count * toks
        scratch += [pltpu.VMEM((everyone,) + small.shape, F32), dma((everyone,)), dma((everyone,))]
        out_shape.append(jax.ShapeDtypeStruct(small.shape, F32))
        operands.append(small)
    return pl.pallas_call(
        functools.partial(scatter_kernel, rows, cols, toks, small is not None),
        out_shape=out_shape,
        in_specs=[VMEM_SPEC] * len(operands),
        out_specs=[VMEM_SPEC] * len(out_shape),
        scratch_shapes=scratch,
        compiler_params=pltpu.CompilerParams(
            collective_id=collective_id, has_side_effects=True, vmem_limit_bytes=48 << 20),
        name=f"scatter{collective_id}",
    )(*operands)


def dot(a, b, ca, cb):
    return lax.dot_general(a, b, (((ca,), (cb,)), ((), ())), preferred_element_type=F32)


def attention_kernel(scale, tiled, bias_ref, chain_j_ref, chain_i_ref, q_ref, u_ref, k_ref, v_ref,
                     mixed_ref, dq_ref, dk_ref, dv_ref, ds_ref):
    keys = k_ref.shape[1]
    lanes = q_ref.shape[2]
    size = q_ref.shape[1]
    first_head = lax.broadcasted_iota(jnp.int32, (size, lanes), 1) < lanes // 2

    def spread(packed):
        zero = jnp.zeros_like(packed)
        return jnp.concatenate(
            [jnp.where(first_head, packed, zero), jnp.where(first_head, zero, packed)], axis=0)

    def pick(wide):
        return jnp.where(first_head, wide[:size], wide[size:])

    query = spread(q_ref[0])
    upstream = spread(u_ref[0])
    key = k_ref[0]
    value = v_ref[0]
    bias = (bias_ref[:, 0] if tiled else bias_ref[0]).astype(F32).reshape(keys, lanes)
    reward = jnp.where(chain_j_ref[...] == chain_i_ref[...], CHAIN_REWARD, 0.0)
    scores = dot(key, query, 1, 0) * scale + (bias + reward)
    peak = jnp.max(scores, axis=0, keepdims=True)
    terms = jnp.exp(scores - peak)
    probs = terms * (1.0 / jnp.sum(terms, axis=0, keepdims=True))
    low = probs.astype(BF16)
    prob_grad = dot(value, upstream, 1, 0)
    middle = jnp.sum(probs * prob_grad, axis=0, keepdims=True)
    score_low = (probs * (prob_grad - middle)).astype(BF16)
    mixed_ref[0] = pick(dot(value, low, 0, 0)).astype(BF16)
    dq_ref[0] = (pick(dot(key, score_low, 0, 0)) * scale).astype(BF16)
    dk_ref[0] = (dot(score_low, query, 1, 1) * scale).astype(BF16)
    dv_ref[0] = dot(low, upstream, 1, 1).astype(BF16)
    if tiled:
        ds_ref[:, 0] = score_low.reshape(ds_ref.shape[0], ds_ref.shape[2], lanes)
    else:
        ds_ref[0] = score_low


def attention(scale, bias, chain_j, chain_i, q, u, k, v):
    pairs, size, lanes = q.shape
    keys, wide = k.shape[1:]
    samp_count, _, part, _ = bias.shape
    tiled = part % 16 == 0

    def spec(*tail):
        return pl.BlockSpec((1,) + tail, lambda g: (g, 0, 0))

    if tiled:
        big = pl.BlockSpec((samp_count, 1, part, lanes), lambda g: (0, g, 0, 0))
        ds_shape = bias.shape
    else:
        bias = bias.transpose(1, 0, 2, 3).reshape(pairs, keys, lanes)
        big = spec(keys, lanes)
        ds_shape = bias.shape
    mixed, dq, dk, dv, ds = pl.pallas_call(
        functools.partial(attention_kernel, scale, tiled),
        grid=(pairs,),
        in_specs=[big,
                  pl.BlockSpec((keys, 1), lambda g: (0, 0)),
                  pl.BlockSpec((1, lanes), lambda g: (0, 0)),
                  spec(size, lanes), spec(size, lanes), spec(keys, wide), spec(keys, wide)],
        out_specs=[spec(size, lanes), spec(size, lanes), spec(keys, wide), spec(keys, wide), big],
        out_shape=[jax.ShapeDtypeStruct((pairs, size, lanes), BF16)] * 2
        + [jax.ShapeDtypeStruct((pairs, keys, wide), BF16)] * 2
        + [jax.ShapeDtypeStruct(ds_shape, BF16)],
        compiler_params=pltpu.CompilerParams(vmem_limit_bytes=48 << 20),
        name="attention_backward",
    )(bias, chain_j, chain_i, q, u, k, v)
    if not tiled:
        ds = ds.reshape(pairs, samp_count, part, lanes).transpose(1, 0, 2, 3)
    return mixed, dq, dk, dv, ds


def per_device(acts, out_grad, pair, chain_of_token, w_query, w_key, w_value, w_out, w_pair):
    samples, row_count, width = acts.shape
    assert samples == 1
    heads = w_pair.shape[1]
    size = width // heads
    pairs = heads // 2
    toks = lax.axis_size("tok")
    samp_count = lax.axis_size("samp")
    keys = row_count * toks
    part = pair.shape[1]
    lanes = 2 * row_count
    scale = 1.0 / math.sqrt(size)
    t = lax.axis_index("tok")

    tile = jnp.einsum("ijc,cpa->pjai", pair, w_pair.reshape(-1, pairs, 2),
                      preferred_element_type=F32).astype(BF16).reshape(pairs, part, lanes)
    bias = gather_over_samp(tile, samp_count)

    rows = acts[0]
    grad_rows = out_grad[0]
    kv_local = jnp.stack([
        jnp.dot(rows, w_key, preferred_element_type=F32).astype(BF16),
        jnp.dot(rows, w_value, preferred_element_type=F32).astype(BF16)])
    swap = [(a, (a + 1) % toks) for a in range(toks)]
    kv_other = lax.ppermute(kv_local, "tok", swap)
    kv = jnp.where(t == 0, jnp.concatenate([kv_local, kv_other], 1),
                   jnp.concatenate([kv_other, kv_local], 1))
    kv = kv.reshape(2, keys, pairs, 2 * size).transpose(0, 2, 1, 3)

    def packed(flat_t):
        return flat_t.reshape(pairs, 2, size, row_count).transpose(0, 2, 1, 3).reshape(
            pairs, size, lanes)

    def unpacked(p):
        return p.reshape(pairs, size, 2, row_count).transpose(0, 2, 1, 3).reshape(width, row_count)

    q = packed(dot(w_query, rows, 0, 1).astype(BF16))
    u = packed(dot(w_out, grad_rows, 1, 1).astype(BF16))
    own_chain = lax.dynamic_slice_in_dim(chain_of_token, t * row_count, row_count, 0)
    chain_i = jnp.concatenate([own_chain, own_chain])[None, :]
    mixed, dq, dk, dv, ds = attention(
        scale, bias, chain_of_token[:, None], chain_i, q, u, kv[0], kv[1])

    bias_grad = scatter_over_samp(
        ds.reshape(samp_count, 1, pairs, part, lanes), 1)[0].astype(BF16)
    dkv = jnp.stack([dk, dv]).transpose(0, 2, 1, 3).reshape(2, toks, row_count, width)
    dkv_mine = jnp.where(t == 0, dkv[:, 0], dkv[:, 1])
    dkv_send = jnp.where(t == 0, dkv[:, 1], dkv[:, 0])
    dkv_got = lax.ppermute(dkv_send, "tok", swap)
    dkv_sum = (dkv_mine.astype(F32) + dkv_got.astype(F32)).astype(BF16)
    dk, dv = dkv_sum[0], dkv_sum[1]
    dq_t = unpacked(dq)
    mixed_t = unpacked(mixed)
    act_grad = dot(dq_t, w_query, 0, 1) + dot(dk, w_key, 1, 1) + dot(dv, w_value, 1, 1)
    act_grad = act_grad.astype(BF16)[None]
    stacked = jnp.concatenate([
        dot(rows, dq_t, 0, 1).astype(BF16),
        dot(rows, dk, 0, 0).astype(BF16),
        dot(rows, dv, 0, 0).astype(BF16),
        dot(mixed_t, grad_rows, 1, 0).astype(BF16)], 0)
    grouped = stacked.reshape(samp_count, toks, -1, width)
    by_head = bias_grad.reshape(pairs, part, 2, row_count)
    w_split = w_pair.reshape(-1, pairs, 2)
    pair_grad = jnp.einsum("pjai,cpa->ijc", by_head, w_split, preferred_element_type=F32)
    pair_term = jnp.einsum("ijc,pjai->pac", pair, by_head, preferred_element_type=F32)
    weight_grads, pair_weight = scatter_over_samp(grouped, 2, pair_term.reshape(heads, -1))
    return act_grad, pair_grad, weight_grads, pair_weight.T


def solution(mesh):
    in_specs = (
        P(("job", "samp"), "tok", None),
        P(("job", "samp"), "tok", None),
        P(("job", "tok"), "samp", None),
        P("job"),
        P(),
        P(),
        P(),
        P(),
        P(),
    )
    out_specs = (
        P(("job", "samp"), "tok", None),
        P(("job", "tok"), "samp", None),
        P(("job", "samp", "tok"), None),
        P("job", None),
    )
    return jax.shard_map(
        per_device, mesh=mesh, in_specs=in_specs, out_specs=out_specs, check_vma=False
    )
```

```python
import functools
import math

import jax
import jax.numpy as jnp
from jax import lax
from jax.experimental import pallas as pl
from jax.experimental.pallas import tpu as pltpu
from jax.sharding import PartitionSpec as P

CHAIN_REWARD = 2.0
MESH_ID = pl.DeviceIdType.MESH
F32 = jnp.float32
BF16 = jnp.bfloat16
VMEM_SPEC = pl.BlockSpec(memory_space=pltpu.VMEM)


def grid_place(samp_count):
    cols = 2 if samp_count % 2 == 0 else 1
    return samp_count // cols, cols


def at_samp(z, y, cols):
    return {"samp": z * cols + y}


def greet_line(rows, cols, z, y, extra=()):
    barrier = pltpu.get_barrier_semaphore()

    @pl.when(z > 0)
    def _():
        pl.semaphore_signal(barrier, 1, device_id=at_samp(z - 1, y, cols), device_id_type=MESH_ID)

    @pl.when(z < rows - 1)
    def _():
        pl.semaphore_signal(barrier, 1, device_id=at_samp(z + 1, y, cols), device_id_type=MESH_ID)

    others = list(extra)
    if cols == 2:
        others.append(at_samp(z, 1 - y, cols))
    for other in others:
        pl.semaphore_signal(barrier, 1, device_id=other, device_id_type=MESH_ID)
    count = len(others) + (z > 0).astype(jnp.int32) + (z < rows - 1).astype(jnp.int32)
    pl.semaphore_wait(barrier, count)


def gather_kernel(rows, cols, subs, x_ref, out_ref, right_send, right_recv, left_send, left_recv,
                  side_send, side_recv):
    me = lax.axis_index("samp")
    z, y = me // cols, me % cols
    span = x_ref.shape[0] // subs
    greet_line(rows, cols, z, y)

    def piece(block, c, sub):
        return out_ref.at[block * cols + c, pl.ds(sub * span, span)]

    def send(block, own, sub, send_sem, recv_sem, target):
        return pltpu.make_async_remote_copy(
            src_ref=x_ref.at[pl.ds(sub * span, span)] if own else piece(block, y, sub),
            dst_ref=piece(block, y, sub), send_sem=send_sem, recv_sem=recv_sem,
            device_id=target, device_id_type=MESH_ID)

    def right(step, sub):
        k = step * subs + sub
        return send(z - step, step == 0, sub, right_send.at[k], right_recv.at[k],
                    at_samp(z + 1, y, cols))

    def left(step, sub):
        k = step * subs + sub
        return send(z + step, step == 0, sub, left_send.at[k], left_recv.at[k],
                    at_samp(z - 1, y, cols))

    def side(slot, block, own, sub):
        return send(block, own, sub, side_send.at[slot * subs + sub],
                    side_recv.at[block * subs + sub], at_samp(z, 1 - y, cols))

    def landed(ref, sem):
        pltpu.make_async_copy(ref, ref, sem).wait()

    for sub in range(subs):
        pl.when(z < rows - 1)(lambda: right(0, sub).start())
        pl.when(z > 0)(lambda: left(0, sub).start())
        if cols == 2:
            side(0, z, True, sub).start()
    out_ref[me] = x_ref[...]
    for step in range(1, rows):
        for sub in range(subs):
            @pl.when(z - step >= 0)
            def _():
                landed(piece(z - step, y, sub), right_recv.at[(step - 1) * subs + sub])

                @pl.when(z < rows - 1)
                def _():
                    right(step, sub).start()
                if cols == 2:
                    side(2 * step - 1, z - step, False, sub).start()

            @pl.when(z + step <= rows - 1)
            def _():
                landed(piece(z + step, y, sub), left_recv.at[(step - 1) * subs + sub])

                @pl.when(z > 0)
                def _():
                    left(step, sub).start()
                if cols == 2:
                    side(2 * step, z + step, False, sub).start()

    for step in range(rows):
        for sub in range(subs):
            pl.when((z - step >= 0) & (z < rows - 1))(lambda: right(step, sub).wait_send())
            pl.when((z + step <= rows - 1) & (z > 0))(lambda: left(step, sub).wait_send())
            if cols == 2:
                if step == 0:
                    side(0, z, True, sub).wait_send()
                else:
                    pl.when(z - step >= 0)(
                        lambda: side(2 * step - 1, z - step, False, sub).wait_send())
                    pl.when(z + step <= rows - 1)(
                        lambda: side(2 * step, z + step, False, sub).wait_send())
    if cols == 2:
        for block in range(rows):
            for sub in range(subs):
                landed(piece(block, 1 - y, sub), side_recv.at[block * subs + sub])


def gather_over_samp(x, samp_count):
    rows, cols = grid_place(samp_count)
    subs = 4 if rows <= 4 and x.shape[0] % 4 == 0 else 1
    dma = pltpu.SemaphoreType.DMA
    line = dma((rows * subs,))
    return pl.pallas_call(
        functools.partial(gather_kernel, rows, cols, subs),
        out_shape=jax.ShapeDtypeStruct((samp_count,) + x.shape, x.dtype),
        in_specs=[VMEM_SPEC],
        out_specs=VMEM_SPEC,
        scratch_shapes=[line, line, line, line, dma((2 * rows * subs,)), line],
        compiler_params=pltpu.CompilerParams(
            collective_id=0, has_side_effects=True, vmem_limit_bytes=48 << 20),
        name="bias_gather",
    )(x)


def chunk_order(rows):
    order = []
    for k in range((rows + 1) // 2):
        order.append(rows - 1 - k)
        if k != rows - 1 - k:
            order.append(k)
    return order


def scatter_kernel(rows, cols, toks, subs, small, *refs):
    refs = list(refs)
    x_ref = refs.pop(0)
    small_ref = refs.pop(0) if small else None
    out_ref = refs.pop(0)
    small_out = refs.pop(0) if small else None
    (core_recv, side_buf, side_recv, total, line_buf, right_buf, left_buf,
     core_ss, core_rs, side_ss, side_rs, line_ss, right_rs, left_rs) = refs[:14]
    me = lax.axis_index("samp")
    z, y = me // cols, me % cols
    t = lax.axis_index("tok") if toks == 2 else 0
    samp_count = rows * cols
    if small:
        all_buf, all_ss, all_rs = refs[14:]
        flat = me * toks + t
        everyone = samp_count * toks
        barrier = pltpu.get_barrier_semaphore()
        peers = []
        for step in range(1, everyone):
            peer = lax.rem(flat + step, everyone)
            peers.append({"samp": peer // toks, "tok": peer % toks})
        for peer in peers:
            pl.semaphore_signal(barrier, 1, device_id=peer, device_id_type=MESH_ID)
        pl.semaphore_wait(barrier, everyone - 1)
        small_copies = [
            pltpu.make_async_remote_copy(
                src_ref=small_ref, dst_ref=all_buf.at[k], send_sem=all_ss.at[k],
                recv_sem=all_rs.at[k], device_id=peer, device_id_type=MESH_ID)
            for k, peer in enumerate(peers)]
    else:
        greet_line(rows, cols, z, y)
        small_copies = []

    order = chunk_order(rows)
    work = [(d, sub) for d in order for sub in range(subs)]
    span = out_ref.shape[0] // subs

    def cut(sub):
        return pl.ds(sub * span, span)

    def core_copy(index, sub):
        return pltpu.make_async_remote_copy(
            src_ref=x_ref.at[index, 1 - t, cut(sub)], dst_ref=core_recv.at[index, cut(sub)],
            send_sem=core_ss.at[index * subs + sub], recv_sem=core_rs.at[index * subs + sub],
            device_id={"tok": 1 - t}, device_id_type=MESH_ID)

    def send(src, dst, d, sub, send_sem, recv_sem, target):
        return pltpu.make_async_remote_copy(
            src_ref=src.at[d, cut(sub)], dst_ref=dst.at[d, cut(sub)],
            send_sem=send_sem.at[d * subs + sub], recv_sem=recv_sem.at[d * subs + sub],
            device_id=target, device_id_type=MESH_ID)

    def side_copy(d, sub):
        return send(side_buf, side_recv, d, sub, side_ss, side_rs, at_samp(z, 1 - y, cols))

    def right_copy(d, sub):
        return send(line_buf, right_buf, d, sub, line_ss, right_rs, at_samp(z + 1, y, cols))

    def left_copy(d, sub):
        return send(line_buf, left_buf, d, sub, line_ss, left_rs, at_samp(z - 1, y, cols))

    if toks == 2:
        for d, sub in work:
            if cols == 2:
                core_copy(d * cols + 1 - y, sub).start()
        for d, sub in work:
            core_copy(d * cols + y, sub).start()
    for copy in small_copies:
        copy.start()

    def local_sum(index, sub):
        value = x_ref[index, t, cut(sub)].astype(F32)
        if toks == 2:
            core_copy(index, sub).wait_recv()
            value = value + core_recv[index, cut(sub)].astype(F32)
        return value

    def side_send(d, sub):
        if toks == 2:
            side_buf[d, cut(sub)] = local_sum(d * cols + 1 - y, sub).astype(BF16)
            side_copy(d, sub).start()
        else:
            raw_side(d, sub).start()

    def raw_side(d, sub):
        return pltpu.make_async_remote_copy(
            src_ref=x_ref.at[d * cols + 1 - y, 0, cut(sub)], dst_ref=side_recv.at[d, cut(sub)],
            send_sem=side_ss.at[d * subs + sub], recv_sem=side_rs.at[d * subs + sub],
            device_id=at_samp(z, 1 - y, cols), device_id_type=MESH_ID)

    if cols == 2:
        for d, sub in work:
            side_send(d, sub)
    for d, sub in work:
        value = local_sum(d * cols + y, sub)
        if cols == 2:
            side_copy(d, sub).wait_recv()
            value = value + side_recv[d, cut(sub)].astype(F32)
        total[cut(sub)] = value

        @pl.when(z < d)
        def _():
            @pl.when(z > 0)
            def _():
                right_copy(d, sub).wait_recv()
                line_buf[d, cut(sub)] = (
                    total[cut(sub)] + right_buf[d, cut(sub)].astype(F32)).astype(BF16)

            @pl.when(z == 0)
            def _():
                line_buf[d, cut(sub)] = total[cut(sub)].astype(BF16)
            right_copy(d, sub).start()

        @pl.when(z > d)
        def _():
            @pl.when(z < rows - 1)
            def _():
                left_copy(d, sub).wait_recv()
                line_buf[d, cut(sub)] = (
                    total[cut(sub)] + left_buf[d, cut(sub)].astype(F32)).astype(BF16)

            @pl.when(z == rows - 1)
            def _():
                line_buf[d, cut(sub)] = total[cut(sub)].astype(BF16)
            left_copy(d, sub).start()

        @pl.when(z == d)
        def _():
            out_ref[cut(sub)] = total[cut(sub)]

    for sub in range(subs):
        @pl.when(z > 0)
        def _():
            right_copy(z, sub).wait_recv()
            out_ref[cut(sub)] += right_buf[z, cut(sub)].astype(F32)

        @pl.when(z < rows - 1)
        def _():
            left_copy(z, sub).wait_recv()
            out_ref[cut(sub)] += left_buf[z, cut(sub)].astype(F32)

    if small:
        whole = small_ref[...]
        for k, copy in enumerate(small_copies):
            copy.wait_recv()
            whole = whole + all_buf[k]
        small_out[...] = whole
    for copy in small_copies:
        copy.wait_send()
    for d, sub in work:
        pl.when(z < d)(lambda: right_copy(d, sub).wait_send())
        pl.when(z > d)(lambda: left_copy(d, sub).wait_send())
        if cols == 2:
            side_copy(d, sub).wait_send()
        if toks == 2:
            for c in range(cols):
                core_copy(d * cols + c, sub).wait_send()


def scatter_over_samp(x, collective_id, small=None):
    samp_count, toks = x.shape[:2]
    chunk = x.shape[2:]
    rows, cols = grid_place(samp_count)
    even = chunk[0] % 4 == 0 and (len(chunk) > 2 or chunk[0] % 64 == 0)
    subs = 4 if rows <= 4 and even else 1
    dma = pltpu.SemaphoreType.DMA
    line = pltpu.VMEM((rows,) + chunk, BF16)
    scratch = [
        pltpu.VMEM(((samp_count if toks == 2 else 1),) + chunk, BF16),
        line, line, pltpu.VMEM(chunk, F32), line, line, line,
        dma((samp_count * subs,)), dma((samp_count * subs,))] + [dma((rows * subs,))] * 5
    out_shape = [jax.ShapeDtypeStruct(chunk, F32)]
    operands = [x]
    if small is not None:
        everyone = samp_count * toks
        scratch += [pltpu.VMEM((everyone,) + small.shape, F32), dma((everyone,)), dma((everyone,))]
        out_shape.append(jax.ShapeDtypeStruct(small.shape, F32))
        operands.append(small)
    return pl.pallas_call(
        functools.partial(scatter_kernel, rows, cols, toks, subs, small is not None),
        out_shape=out_shape,
        in_specs=[VMEM_SPEC] * len(operands),
        out_specs=[VMEM_SPEC] * len(out_shape),
        scratch_shapes=scratch,
        compiler_params=pltpu.CompilerParams(
            collective_id=collective_id, has_side_effects=True, vmem_limit_bytes=48 << 20),
        name=f"scatter{collective_id}",
    )(*operands)


def dot(a, b, ca, cb):
    return lax.dot_general(a, b, (((ca,), (cb,)), ((), ())), preferred_element_type=F32)


def attention_kernel(scale, tiled, bias_ref, chain_j_ref, chain_i_ref, q_ref, u_ref,
                     k_own_ref, k_far_ref, v_own_ref, v_far_ref,
                     mixed_ref, dq_ref, dk_own_ref, dk_far_ref, dv_own_ref, dv_far_ref, ds_ref,
                     k_buf, v_buf, dk_buf, dv_buf):
    pairs, size, lanes = q_ref.shape
    half = k_own_ref.shape[0]
    keys = k_buf.shape[0]
    t = lax.axis_index("tok")
    if keys == half:
        own = far = pl.ds(0, half)
    else:
        own, far = pl.ds(t * half, half), pl.ds((1 - t) * half, half)
    k_buf[far] = k_far_ref[...]
    v_buf[far] = v_far_ref[...]
    k_buf[own] = k_own_ref[...]
    v_buf[own] = v_own_ref[...]
    first_head = lax.broadcasted_iota(jnp.int32, (size, lanes), 1) < lanes // 2

    def spread(packed):
        zero = jnp.zeros_like(packed)
        return jnp.concatenate(
            [jnp.where(first_head, packed, zero), jnp.where(first_head, zero, packed)], axis=0)

    def pick(wide):
        return jnp.where(first_head, wide[:size], wide[size:])

    for g in range(pairs):
        span = slice(2 * size * g, 2 * size * (g + 1))
        query = spread(q_ref[g])
        upstream = spread(u_ref[g])
        key = k_buf[:, span]
        value = v_buf[:, span]
        bias = (bias_ref[:, g] if tiled else bias_ref[g]).astype(F32).reshape(keys, lanes)
        reward = jnp.where(chain_j_ref[...] == chain_i_ref[...], CHAIN_REWARD, 0.0)
        scores = dot(key, query, 1, 0) * scale + (bias + reward)
        peak = jnp.max(scores, axis=0, keepdims=True)
        terms = jnp.exp(scores - peak)
        probs = terms * (1.0 / jnp.sum(terms, axis=0, keepdims=True))
        low = probs.astype(BF16)
        prob_grad = dot(value, upstream, 1, 0)
        middle = jnp.sum(probs * prob_grad, axis=0, keepdims=True)
        score_low = (probs * (prob_grad - middle)).astype(BF16)
        mixed_ref[g] = pick(dot(value, low, 0, 0)).astype(BF16)
        dq_ref[g] = (pick(dot(key, score_low, 0, 0)) * scale).astype(BF16)
        dk_buf[:, span] = (dot(score_low, query, 1, 1) * scale).astype(BF16)
        dv_buf[:, span] = dot(low, upstream, 1, 1).astype(BF16)
        if tiled:
            ds_ref[:, g] = score_low.reshape(ds_ref.shape[0], ds_ref.shape[2], lanes)
        else:
            ds_ref[g] = score_low
    dk_own_ref[...] = dk_buf[own]
    dk_far_ref[...] = dk_buf[far]
    dv_own_ref[...] = dv_buf[own]
    dv_far_ref[...] = dv_buf[far]


def attention(scale, bias, chain_j, chain_i, q, u, k_own, k_far, v_own, v_far):
    pairs, size, lanes = q.shape
    half, width = k_own.shape
    keys = chain_j.shape[0]
    samp_count, _, part, _ = bias.shape
    tiled = part % 16 == 0
    if not tiled:
        bias = bias.transpose(1, 0, 2, 3).reshape(pairs, keys, lanes)
    packed = jax.ShapeDtypeStruct((pairs, size, lanes), BF16)
    flat = jax.ShapeDtypeStruct((half, width), BF16)
    *grads, ds = pl.pallas_call(
        functools.partial(attention_kernel, scale, tiled),
        in_specs=[VMEM_SPEC] * 9,
        out_specs=[VMEM_SPEC] * 7,
        out_shape=[packed] * 2 + [flat] * 4 + [jax.ShapeDtypeStruct(bias.shape, BF16)],
        scratch_shapes=[pltpu.VMEM((keys, width), BF16)] * 4,
        compiler_params=pltpu.CompilerParams(vmem_limit_bytes=48 << 20),
        name="attention_backward",
    )(bias, chain_j, chain_i, q, u, k_own, k_far, v_own, v_far)
    if not tiled:
        ds = ds.reshape(pairs, samp_count, part, lanes).transpose(1, 0, 2, 3)
    return (*grads, ds)


def per_device(acts, out_grad, pair, chain_of_token, w_query, w_key, w_value, w_out, w_pair):
    samples, row_count, width = acts.shape
    assert samples == 1
    heads = w_pair.shape[1]
    size = width // heads
    pairs = heads // 2
    toks = lax.axis_size("tok")
    samp_count = lax.axis_size("samp")
    keys = row_count * toks
    part = pair.shape[1]
    lanes = 2 * row_count
    scale = 1.0 / math.sqrt(size)
    t = lax.axis_index("tok")

    tile = jnp.einsum("ijc,cpa->pjai", pair, w_pair.reshape(-1, pairs, 2),
                      preferred_element_type=F32).astype(BF16).reshape(pairs, part, lanes)
    bias = gather_over_samp(tile, samp_count)

    rows = acts[0]
    grad_rows = out_grad[0]
    k_own = jnp.dot(rows, w_key, preferred_element_type=F32).astype(BF16)
    v_own = jnp.dot(rows, w_value, preferred_element_type=F32).astype(BF16)
    swap = [(a, (a + 1) % toks) for a in range(toks)]
    k_far = lax.ppermute(k_own, "tok", swap)
    v_far = lax.ppermute(v_own, "tok", swap)

    def packed(flat_t):
        return flat_t.reshape(pairs, 2, size, row_count).transpose(0, 2, 1, 3).reshape(
            pairs, size, lanes)

    def unpacked(p):
        return p.reshape(pairs, size, 2, row_count).transpose(0, 2, 1, 3).reshape(width, row_count)

    q = packed(dot(w_query, rows, 0, 1).astype(BF16))
    u = packed(dot(w_out, grad_rows, 1, 1).astype(BF16))
    own_chain = lax.dynamic_slice_in_dim(chain_of_token, t * row_count, row_count, 0)
    chain_i = jnp.concatenate([own_chain, own_chain])[None, :]
    mixed, dq, dk_own, dk_far, dv_own, dv_far, ds = attention(
        scale, bias, chain_of_token[:, None], chain_i, q, u, k_own, k_far, v_own, v_far)

    bias_grad = scatter_over_samp(
        ds.reshape(samp_count, 1, pairs, part, lanes), 1)[0].astype(BF16)

    def summed(mine, sent):
        if toks == 1:
            return mine
        return (mine.astype(F32) + lax.ppermute(sent, "tok", swap).astype(F32)).astype(BF16)

    dk = summed(dk_own, dk_far)
    dv = summed(dv_own, dv_far)
    dq_t = unpacked(dq)
    mixed_t = unpacked(mixed)
    act_grad = dot(dq_t, w_query, 0, 1) + dot(dk, w_key, 1, 1) + dot(dv, w_value, 1, 1)
    act_grad = act_grad.astype(BF16)[None]
    stacked = jnp.concatenate([
        dot(rows, dq_t, 0, 1).astype(BF16),
        dot(rows, dk, 0, 0).astype(BF16),
        dot(rows, dv, 0, 0).astype(BF16),
        dot(mixed_t, grad_rows, 1, 0).astype(BF16)], 0)
    grouped = stacked.reshape(samp_count, toks, -1, width)
    by_head = bias_grad.reshape(pairs, part, 2, row_count).transpose(3, 1, 0, 2)
    by_head = lax.optimization_barrier(by_head.reshape(row_count * part, heads))
    pair_grad = dot(by_head, w_pair, 1, 1).reshape(pair.shape)
    pair_term = dot(by_head, pair.reshape(row_count * part, -1), 0, 0)
    weight_grads, pair_weight = scatter_over_samp(grouped, 2, pair_term)
    return act_grad, pair_grad, weight_grads, pair_weight.T


def solution(mesh):
    in_specs = (
        P(("job", "samp"), "tok", None),
        P(("job", "samp"), "tok", None),
        P(("job", "tok"), "samp", None),
        P("job"),
        P(),
        P(),
        P(),
        P(),
        P(),
    )
    out_specs = (
        P(("job", "samp"), "tok", None),
        P(("job", "tok"), "samp", None),
        P(("job", "samp", "tok"), None),
        P("job", None),
    )
    return jax.shard_map(
        per_device, mesh=mesh, in_specs=in_specs, out_specs=out_specs, check_vma=False
    )
```

```python
import functools
import math

import jax
import jax.numpy as jnp
from jax import lax
from jax.experimental import pallas as pl
from jax.experimental.pallas import tpu as pltpu
from jax.sharding import PartitionSpec as P

CHAIN_REWARD = 2.0
MESH_ID = pl.DeviceIdType.MESH
F32 = jnp.float32
BF16 = jnp.bfloat16
VMEM_SPEC = pl.BlockSpec(memory_space=pltpu.VMEM)


def grid_place(samp_count):
    cols = 2 if samp_count % 2 == 0 else 1
    return samp_count // cols, cols


def at_samp(z, y, cols):
    return {"samp": z * cols + y}


def greet_line(rows, cols, z, y, extra=()):
    barrier = pltpu.get_barrier_semaphore()

    @pl.when(z > 0)
    def _():
        pl.semaphore_signal(barrier, 1, device_id=at_samp(z - 1, y, cols), device_id_type=MESH_ID)

    @pl.when(z < rows - 1)
    def _():
        pl.semaphore_signal(barrier, 1, device_id=at_samp(z + 1, y, cols), device_id_type=MESH_ID)

    others = list(extra)
    if cols == 2:
        others.append(at_samp(z, 1 - y, cols))
    for other in others:
        pl.semaphore_signal(barrier, 1, device_id=other, device_id_type=MESH_ID)
    count = len(others) + (z > 0).astype(jnp.int32) + (z < rows - 1).astype(jnp.int32)
    pl.semaphore_wait(barrier, count)


def gather_kernel(rows, cols, subs, x_ref, out_ref, right_send, right_recv, left_send, left_recv,
                  side_send, side_recv):
    me = lax.axis_index("samp")
    z, y = me // cols, me % cols
    span = x_ref.shape[0] // subs
    greet_line(rows, cols, z, y)

    def piece(block, c, sub):
        return out_ref.at[block * cols + c, pl.ds(sub * span, span)]

    def send(block, own, sub, send_sem, recv_sem, target):
        return pltpu.make_async_remote_copy(
            src_ref=x_ref.at[pl.ds(sub * span, span)] if own else piece(block, y, sub),
            dst_ref=piece(block, y, sub), send_sem=send_sem, recv_sem=recv_sem,
            device_id=target, device_id_type=MESH_ID)

    def right(step, sub):
        k = step * subs + sub
        return send(z - step, step == 0, sub, right_send.at[k], right_recv.at[k],
                    at_samp(z + 1, y, cols))

    def left(step, sub):
        k = step * subs + sub
        return send(z + step, step == 0, sub, left_send.at[k], left_recv.at[k],
                    at_samp(z - 1, y, cols))

    def side(slot, block, own, sub):
        return send(block, own, sub, side_send.at[slot * subs + sub],
                    side_recv.at[block * subs + sub], at_samp(z, 1 - y, cols))

    def landed(ref, sem):
        pltpu.make_async_copy(ref, ref, sem).wait()

    for sub in range(subs):
        pl.when(z < rows - 1)(lambda: right(0, sub).start())
        pl.when(z > 0)(lambda: left(0, sub).start())
        if cols == 2:
            side(0, z, True, sub).start()
    out_ref[me] = x_ref[...]
    for step in range(1, rows):
        for sub in range(subs):
            @pl.when(z - step >= 0)
            def _():
                landed(piece(z - step, y, sub), right_recv.at[(step - 1) * subs + sub])

                @pl.when(z < rows - 1)
                def _():
                    right(step, sub).start()
                if cols == 2:
                    side(2 * step - 1, z - step, False, sub).start()

            @pl.when(z + step <= rows - 1)
            def _():
                landed(piece(z + step, y, sub), left_recv.at[(step - 1) * subs + sub])

                @pl.when(z > 0)
                def _():
                    left(step, sub).start()
                if cols == 2:
                    side(2 * step, z + step, False, sub).start()

    for step in range(rows):
        for sub in range(subs):
            pl.when((z - step >= 0) & (z < rows - 1))(lambda: right(step, sub).wait_send())
            pl.when((z + step <= rows - 1) & (z > 0))(lambda: left(step, sub).wait_send())
            if cols == 2:
                if step == 0:
                    side(0, z, True, sub).wait_send()
                else:
                    pl.when(z - step >= 0)(
                        lambda: side(2 * step - 1, z - step, False, sub).wait_send())
                    pl.when(z + step <= rows - 1)(
                        lambda: side(2 * step, z + step, False, sub).wait_send())
    if cols == 2:
        for block in range(rows):
            for sub in range(subs):
                landed(piece(block, 1 - y, sub), side_recv.at[block * subs + sub])


def gather_over_samp(x, samp_count):
    rows, cols = grid_place(samp_count)
    subs = 4 if rows <= 4 and x.shape[0] % 4 == 0 else 1
    dma = pltpu.SemaphoreType.DMA
    line = dma((rows * subs,))
    return pl.pallas_call(
        functools.partial(gather_kernel, rows, cols, subs),
        out_shape=jax.ShapeDtypeStruct((samp_count,) + x.shape, x.dtype),
        in_specs=[VMEM_SPEC],
        out_specs=VMEM_SPEC,
        scratch_shapes=[line, line, line, line, dma((2 * rows * subs,)), line],
        compiler_params=pltpu.CompilerParams(
            collective_id=0, has_side_effects=True, vmem_limit_bytes=48 << 20),
        name="bias_gather",
    )(x)


def chunk_order(rows):
    order = []
    for k in range((rows + 1) // 2):
        order.append(rows - 1 - k)
        if k != rows - 1 - k:
            order.append(k)
    return order


def scatter_stream(rows, cols, toks, subs, z, y, t, x_ref, out_ref, scratch):
    (core_recv, side_buf, side_recv, total, line_buf, right_buf, left_buf,
     core_ss, core_rs, side_ss, side_rs, line_ss, right_rs, left_rs) = scratch
    order = chunk_order(rows)
    work = [(d, sub) for d in order for sub in range(subs)]
    span = out_ref.shape[0] // subs

    def cut(sub):
        return pl.ds(sub * span, span)

    def core_copy(index, sub):
        return pltpu.make_async_remote_copy(
            src_ref=x_ref.at[index, 1 - t, cut(sub)], dst_ref=core_recv.at[index, cut(sub)],
            send_sem=core_ss.at[index * subs + sub], recv_sem=core_rs.at[index * subs + sub],
            device_id={"tok": 1 - t}, device_id_type=MESH_ID)

    def send(src, dst, d, sub, send_sem, recv_sem, target):
        return pltpu.make_async_remote_copy(
            src_ref=src.at[d, cut(sub)], dst_ref=dst.at[d, cut(sub)],
            send_sem=send_sem.at[d * subs + sub], recv_sem=recv_sem.at[d * subs + sub],
            device_id=target, device_id_type=MESH_ID)

    def side_copy(d, sub):
        return send(side_buf, side_recv, d, sub, side_ss, side_rs, at_samp(z, 1 - y, cols))

    def right_copy(d, sub):
        return send(line_buf, right_buf, d, sub, line_ss, right_rs, at_samp(z + 1, y, cols))

    def left_copy(d, sub):
        return send(line_buf, left_buf, d, sub, line_ss, left_rs, at_samp(z - 1, y, cols))

    def local_sum(index, sub):
        value = x_ref[index, t, cut(sub)].astype(F32)
        if toks == 2:
            core_copy(index, sub).wait_recv()
            value = value + core_recv[index, cut(sub)].astype(F32)
        return value

    def side_send(d, sub):
        if toks == 2:
            side_buf[d, cut(sub)] = local_sum(d * cols + 1 - y, sub).astype(BF16)
            side_copy(d, sub).start()
        else:
            raw_side(d, sub).start()

    def raw_side(d, sub):
        return pltpu.make_async_remote_copy(
            src_ref=x_ref.at[d * cols + 1 - y, 0, cut(sub)], dst_ref=side_recv.at[d, cut(sub)],
            send_sem=side_ss.at[d * subs + sub], recv_sem=side_rs.at[d * subs + sub],
            device_id=at_samp(z, 1 - y, cols), device_id_type=MESH_ID)

    def start_core():
        if toks == 2:
            for d, sub in work:
                if cols == 2:
                    core_copy(d * cols + 1 - y, sub).start()
            for d, sub in work:
                core_copy(d * cols + y, sub).start()

    def start_side():
        if cols == 2:
            for d, sub in work:
                side_send(d, sub)

    def along_line():
        for d, sub in work:
            value = local_sum(d * cols + y, sub)
            if cols == 2:
                side_copy(d, sub).wait_recv()
                value = value + side_recv[d, cut(sub)].astype(F32)
            total[cut(sub)] = value

            @pl.when(z < d)
            def _():
                @pl.when(z > 0)
                def _():
                    right_copy(d, sub).wait_recv()
                    line_buf[d, cut(sub)] = (
                        total[cut(sub)] + right_buf[d, cut(sub)].astype(F32)).astype(BF16)

                @pl.when(z == 0)
                def _():
                    line_buf[d, cut(sub)] = total[cut(sub)].astype(BF16)
                right_copy(d, sub).start()

            @pl.when(z > d)
            def _():
                @pl.when(z < rows - 1)
                def _():
                    left_copy(d, sub).wait_recv()
                    line_buf[d, cut(sub)] = (
                        total[cut(sub)] + left_buf[d, cut(sub)].astype(F32)).astype(BF16)

                @pl.when(z == rows - 1)
                def _():
                    line_buf[d, cut(sub)] = total[cut(sub)].astype(BF16)
                left_copy(d, sub).start()

            @pl.when(z == d)
            def _():
                out_ref[cut(sub)] = total[cut(sub)]

    def finish():
        for sub in range(subs):
            @pl.when(z > 0)
            def _():
                right_copy(z, sub).wait_recv()
                out_ref[cut(sub)] += right_buf[z, cut(sub)].astype(F32)

            @pl.when(z < rows - 1)
            def _():
                left_copy(z, sub).wait_recv()
                out_ref[cut(sub)] += left_buf[z, cut(sub)].astype(F32)

    def drain():
        for d, sub in work:
            pl.when(z < d)(lambda: right_copy(d, sub).wait_send())
            pl.when(z > d)(lambda: left_copy(d, sub).wait_send())
            if cols == 2:
                side_copy(d, sub).wait_send()
            if toks == 2:
                for c in range(cols):
                    core_copy(d * cols + c, sub).wait_send()

    return start_core, start_side, along_line, finish, drain


def scatter_kernel(rows, cols, toks, subs, *refs):
    count = len(toks)
    me = lax.axis_index("samp")
    z, y = me // cols, me % cols
    t = lax.axis_index("tok")
    greet_line(rows, cols, z, y, [{"tok": 1 - t}] if 2 in toks else [])
    streams = []
    for k in range(count):
        scratch = refs[2 * count + 14 * k:2 * count + 14 * (k + 1)]
        streams.append(scatter_stream(
            rows, cols, toks[k], subs[k], z, y, t if toks[k] == 2 else 0,
            refs[k], refs[count + k], scratch))
    for phase in zip(*streams):
        for part in phase:
            part()


def scatter_scratch(x, rows, subs):
    samp_count, toks = x.shape[:2]
    chunk = x.shape[2:]
    dma = pltpu.SemaphoreType.DMA
    line = pltpu.VMEM((rows,) + chunk, BF16)
    return [
        pltpu.VMEM(((samp_count if toks == 2 else 1),) + chunk, BF16),
        line, line, pltpu.VMEM(chunk, F32), line, line, line,
        dma((samp_count * subs,)), dma((samp_count * subs,))] + [dma((rows * subs,))] * 5


def scatter_over_samp(*arrays):
    rows, cols = grid_place(arrays[0].shape[0])
    subs = []
    scratch = []
    for x in arrays:
        chunk = x.shape[2:]
        even = chunk[0] % 4 == 0 and (len(chunk) > 2 or chunk[0] % 64 == 0)
        subs.append(4 if rows <= 4 and even else 1)
        scratch += scatter_scratch(x, rows, subs[-1])
    return pl.pallas_call(
        functools.partial(
            scatter_kernel, rows, cols, tuple(x.shape[1] for x in arrays), tuple(subs)),
        out_shape=[jax.ShapeDtypeStruct(x.shape[2:], F32) for x in arrays],
        in_specs=[VMEM_SPEC] * len(arrays),
        out_specs=[VMEM_SPEC] * len(arrays),
        scratch_shapes=scratch,
        compiler_params=pltpu.CompilerParams(
            collective_id=1, has_side_effects=True, vmem_limit_bytes=56 << 20),
        name="gradient_scatter",
    )(*arrays)


def small_sum_kernel(samp_count, toks, x_ref, out_ref, all_buf, send_sem, recv_sem):
    everyone = samp_count * toks
    flat = lax.axis_index("samp") * toks + lax.axis_index("tok")
    barrier = pltpu.get_barrier_semaphore()
    copies = []
    for step in range(1, everyone):
        peer = lax.rem(flat + step, everyone)
        target = {"samp": peer // toks, "tok": peer % toks}
        pl.semaphore_signal(barrier, 1, device_id=target, device_id_type=MESH_ID)
        copies.append(pltpu.make_async_remote_copy(
            src_ref=x_ref, dst_ref=all_buf.at[step - 1], send_sem=send_sem.at[step - 1],
            recv_sem=recv_sem.at[step - 1], device_id=target, device_id_type=MESH_ID))
    pl.semaphore_wait(barrier, everyone - 1)
    for copy in copies:
        copy.start()
    whole = x_ref[...]
    for k, copy in enumerate(copies):
        copy.wait_recv()
        whole = whole + all_buf[k]
    out_ref[...] = whole
    for copy in copies:
        copy.wait_send()


def small_sum(x, samp_count, toks):
    everyone = samp_count * toks
    dma = pltpu.SemaphoreType.DMA
    return pl.pallas_call(
        functools.partial(small_sum_kernel, samp_count, toks),
        out_shape=jax.ShapeDtypeStruct(x.shape, F32),
        in_specs=[VMEM_SPEC],
        out_specs=VMEM_SPEC,
        scratch_shapes=[pltpu.VMEM((everyone,) + x.shape, F32), dma((everyone,)),
                        dma((everyone,))],
        compiler_params=pltpu.CompilerParams(collective_id=2, has_side_effects=True),
        name="small_sum",
    )(x)


def dot(a, b, ca, cb):
    return lax.dot_general(a, b, (((ca,), (cb,)), ((), ())), preferred_element_type=F32)


def attention_kernel(scale, tiled, bias_ref, chain_j_ref, chain_i_ref, q_ref, u_ref,
                     k_own_ref, k_far_ref, v_own_ref, v_far_ref,
                     mixed_ref, dq_ref, dk_own_ref, dk_far_ref, dv_own_ref, dv_far_ref, ds_ref,
                     k_buf, v_buf, dk_buf, dv_buf):
    pairs, size, lanes = q_ref.shape
    half = k_own_ref.shape[0]
    keys = k_buf.shape[0]
    t = lax.axis_index("tok")
    if keys == half:
        own = far = pl.ds(0, half)
    else:
        own, far = pl.ds(t * half, half), pl.ds((1 - t) * half, half)
    k_buf[far] = k_far_ref[...]
    v_buf[far] = v_far_ref[...]
    k_buf[own] = k_own_ref[...]
    v_buf[own] = v_own_ref[...]
    first_head = lax.broadcasted_iota(jnp.int32, (size, lanes), 1) < lanes // 2

    def spread(packed):
        zero = jnp.zeros_like(packed)
        return jnp.concatenate(
            [jnp.where(first_head, packed, zero), jnp.where(first_head, zero, packed)], axis=0)

    def pick(wide):
        return jnp.where(first_head, wide[:size], wide[size:])

    for g in range(pairs):
        span = slice(2 * size * g, 2 * size * (g + 1))
        query = spread(q_ref[g])
        upstream = spread(u_ref[g])
        key = k_buf[:, span]
        value = v_buf[:, span]
        bias = (bias_ref[:, g] if tiled else bias_ref[g]).astype(F32).reshape(keys, lanes)
        reward = jnp.where(chain_j_ref[...] == chain_i_ref[...], CHAIN_REWARD, 0.0)
        scores = dot(key, query, 1, 0) * scale + (bias + reward)
        peak = jnp.max(scores, axis=0, keepdims=True)
        terms = jnp.exp(scores - peak)
        probs = terms * (1.0 / jnp.sum(terms, axis=0, keepdims=True))
        low = probs.astype(BF16)
        prob_grad = dot(value, upstream, 1, 0)
        middle = jnp.sum(probs * prob_grad, axis=0, keepdims=True)
        score_low = (probs * (prob_grad - middle)).astype(BF16)
        mixed_ref[g] = pick(dot(value, low, 0, 0)).astype(BF16)
        dq_ref[g] = (pick(dot(key, score_low, 0, 0)) * scale).astype(BF16)
        dk_buf[:, span] = (dot(score_low, query, 1, 1) * scale).astype(BF16)
        dv_buf[:, span] = dot(low, upstream, 1, 1).astype(BF16)
        if tiled:
            ds_ref[:, g] = score_low.reshape(ds_ref.shape[0], ds_ref.shape[2], lanes)
        else:
            ds_ref[g] = score_low
    dk_own_ref[...] = dk_buf[own]
    dk_far_ref[...] = dk_buf[far]
    dv_own_ref[...] = dv_buf[own]
    dv_far_ref[...] = dv_buf[far]


def attention(scale, bias, chain_j, chain_i, q, u, k_own, k_far, v_own, v_far):
    pairs, size, lanes = q.shape
    half, width = k_own.shape
    keys = chain_j.shape[0]
    samp_count, _, part, _ = bias.shape
    tiled = part % 16 == 0
    if not tiled:
        bias = bias.transpose(1, 0, 2, 3).reshape(pairs, keys, lanes)
    packed = jax.ShapeDtypeStruct((pairs, size, lanes), BF16)
    flat = jax.ShapeDtypeStruct((half, width), BF16)
    *grads, ds = pl.pallas_call(
        functools.partial(attention_kernel, scale, tiled),
        in_specs=[pl.BlockSpec()] * 9,
        out_specs=[pl.BlockSpec()] * 7,
        out_shape=[packed] * 2 + [flat] * 4 + [jax.ShapeDtypeStruct(bias.shape, BF16)],
        scratch_shapes=[pltpu.VMEM((keys, width), BF16)] * 4,
        compiler_params=pltpu.CompilerParams(vmem_limit_bytes=48 << 20),
        name="attention_backward",
    )(bias, chain_j, chain_i, q, u, k_own, k_far, v_own, v_far)
    if not tiled:
        ds = ds.reshape(pairs, samp_count, part, lanes).transpose(1, 0, 2, 3)
    return (*grads, ds)


def per_device(acts, out_grad, pair, chain_of_token, w_query, w_key, w_value, w_out, w_pair):
    samples, row_count, width = acts.shape
    assert samples == 1
    heads = w_pair.shape[1]
    size = width // heads
    pairs = heads // 2
    toks = lax.axis_size("tok")
    samp_count = lax.axis_size("samp")
    keys = row_count * toks
    part = pair.shape[1]
    lanes = 2 * row_count
    scale = 1.0 / math.sqrt(size)
    t = lax.axis_index("tok")

    tile = jnp.einsum("ijc,cpa->pjai", pair, w_pair.reshape(-1, pairs, 2),
                      preferred_element_type=F32).astype(BF16).reshape(pairs, part, lanes)
    bias = gather_over_samp(tile, samp_count)

    rows = acts[0]
    grad_rows = out_grad[0]
    k_own = jnp.dot(rows, w_key, preferred_element_type=F32).astype(BF16)
    v_own = jnp.dot(rows, w_value, preferred_element_type=F32).astype(BF16)
    swap = [(a, (a + 1) % toks) for a in range(toks)]
    k_far = lax.ppermute(k_own, "tok", swap)
    v_far = lax.ppermute(v_own, "tok", swap)

    def packed(flat_t):
        return flat_t.reshape(pairs, 2, size, row_count).transpose(0, 2, 1, 3).reshape(
            pairs, size, lanes)

    def unpacked(p):
        return p.reshape(pairs, size, 2, row_count).transpose(0, 2, 1, 3).reshape(width, row_count)

    q = packed(dot(w_query, rows, 0, 1).astype(BF16))
    u = packed(dot(w_out, grad_rows, 1, 1).astype(BF16))
    own_chain = lax.dynamic_slice_in_dim(chain_of_token, t * row_count, row_count, 0)
    chain_i = jnp.concatenate([own_chain, own_chain])[None, :]
    mixed, dq, dk_own, dk_far, dv_own, dv_far, ds = attention(
        scale, bias, chain_of_token[:, None], chain_i, q, u, k_own, k_far, v_own, v_far)

    def summed(mine, sent):
        if toks == 1:
            return mine
        return (mine.astype(F32) + lax.ppermute(sent, "tok", swap).astype(F32)).astype(BF16)

    dk = summed(dk_own, dk_far)
    dv = summed(dv_own, dv_far)
    dq_t = unpacked(dq)
    mixed_t = unpacked(mixed)
    act_grad = dot(dq_t, w_query, 0, 1) + dot(dk, w_key, 1, 1) + dot(dv, w_value, 1, 1)
    act_grad = act_grad.astype(BF16)[None]
    stacked = jnp.concatenate([
        dot(rows, dq_t, 0, 1).astype(BF16),
        dot(rows, dk, 0, 0).astype(BF16),
        dot(rows, dv, 0, 0).astype(BF16),
        dot(mixed_t, grad_rows, 1, 0).astype(BF16)], 0)
    grouped = stacked.reshape(samp_count, toks, -1, width)
    bias_grad, weight_grads = scatter_over_samp(
        ds.reshape(samp_count, 1, pairs, part, lanes), grouped)
    by_head = bias_grad.astype(BF16).reshape(pairs, part, 2, row_count).transpose(3, 1, 0, 2)
    by_head = lax.optimization_barrier(by_head.reshape(row_count * part, heads))
    pair_grad = dot(by_head, w_pair, 1, 1).reshape(pair.shape)
    pair_term = dot(by_head, pair.reshape(row_count * part, -1), 0, 0)
    pair_weight = small_sum(pair_term, samp_count, toks)
    return act_grad, pair_grad, weight_grads, pair_weight.T


def solution(mesh):
    in_specs = (
        P(("job", "samp"), "tok", None),
        P(("job", "samp"), "tok", None),
        P(("job", "tok"), "samp", None),
        P("job"),
        P(),
        P(),
        P(),
        P(),
        P(),
    )
    out_specs = (
        P(("job", "samp"), "tok", None),
        P(("job", "tok"), "samp", None),
        P(("job", "samp", "tok"), None),
        P("job", None),
    )
    return jax.shard_map(
        per_device, mesh=mesh, in_specs=in_specs, out_specs=out_specs, check_vma=False
    )
```

```python
import functools
import math

import jax
import jax.numpy as jnp
from jax import lax
from jax.experimental import pallas as pl
from jax.experimental.pallas import tpu as pltpu
from jax.sharding import PartitionSpec as P

CHAIN_REWARD = 2.0
MESH_ID = pl.DeviceIdType.MESH
F32 = jnp.float32
BF16 = jnp.bfloat16
VMEM_SPEC = pl.BlockSpec(memory_space=pltpu.VMEM)


def grid_place(samp_count):
    cols = 2 if samp_count % 2 == 0 else 1
    return samp_count // cols, cols


def at_samp(z, y, cols):
    return {"samp": z * cols + y}


def greet_line(rows, cols, z, y, extra=()):
    barrier = pltpu.get_barrier_semaphore()

    @pl.when(z > 0)
    def _():
        pl.semaphore_signal(barrier, 1, device_id=at_samp(z - 1, y, cols), device_id_type=MESH_ID)

    @pl.when(z < rows - 1)
    def _():
        pl.semaphore_signal(barrier, 1, device_id=at_samp(z + 1, y, cols), device_id_type=MESH_ID)

    others = list(extra)
    if cols == 2:
        others.append(at_samp(z, 1 - y, cols))
    for other in others:
        pl.semaphore_signal(barrier, 1, device_id=other, device_id_type=MESH_ID)
    count = len(others) + (z > 0).astype(jnp.int32) + (z < rows - 1).astype(jnp.int32)
    pl.semaphore_wait(barrier, count)


def gather_kernel(rows, cols, subs, x_ref, out_ref, right_send, right_recv, left_send, left_recv,
                  side_send, side_recv):
    me = lax.axis_index("samp")
    z, y = me // cols, me % cols
    span = x_ref.shape[0] // subs
    greet_line(rows, cols, z, y)

    def piece(block, c, sub):
        return out_ref.at[block * cols + c, pl.ds(sub * span, span)]

    def send(block, own, sub, send_sem, recv_sem, target):
        return pltpu.make_async_remote_copy(
            src_ref=x_ref.at[pl.ds(sub * span, span)] if own else piece(block, y, sub),
            dst_ref=piece(block, y, sub), send_sem=send_sem, recv_sem=recv_sem,
            device_id=target, device_id_type=MESH_ID)

    def right(step, sub):
        k = step * subs + sub
        return send(z - step, step == 0, sub, right_send.at[k], right_recv.at[k],
                    at_samp(z + 1, y, cols))

    def left(step, sub):
        k = step * subs + sub
        return send(z + step, step == 0, sub, left_send.at[k], left_recv.at[k],
                    at_samp(z - 1, y, cols))

    def side(slot, block, own, sub):
        return send(block, own, sub, side_send.at[slot * subs + sub],
                    side_recv.at[block * subs + sub], at_samp(z, 1 - y, cols))

    def landed(ref, sem):
        pltpu.make_async_copy(ref, ref, sem).wait()

    for sub in range(subs):
        pl.when(z < rows - 1)(lambda: right(0, sub).start())
        pl.when(z > 0)(lambda: left(0, sub).start())
        if cols == 2:
            side(0, z, True, sub).start()
    out_ref[me] = x_ref[...]
    for step in range(1, rows):
        for sub in range(subs):
            @pl.when(z - step >= 0)
            def _():
                landed(piece(z - step, y, sub), right_recv.at[(step - 1) * subs + sub])

                @pl.when(z < rows - 1)
                def _():
                    right(step, sub).start()
                if cols == 2:
                    side(2 * step - 1, z - step, False, sub).start()

            @pl.when(z + step <= rows - 1)
            def _():
                landed(piece(z + step, y, sub), left_recv.at[(step - 1) * subs + sub])

                @pl.when(z > 0)
                def _():
                    left(step, sub).start()
                if cols == 2:
                    side(2 * step, z + step, False, sub).start()

    for step in range(rows):
        for sub in range(subs):
            pl.when((z - step >= 0) & (z < rows - 1))(lambda: right(step, sub).wait_send())
            pl.when((z + step <= rows - 1) & (z > 0))(lambda: left(step, sub).wait_send())
            if cols == 2:
                if step == 0:
                    side(0, z, True, sub).wait_send()
                else:
                    pl.when(z - step >= 0)(
                        lambda: side(2 * step - 1, z - step, False, sub).wait_send())
                    pl.when(z + step <= rows - 1)(
                        lambda: side(2 * step, z + step, False, sub).wait_send())
    if cols == 2:
        for block in range(rows):
            for sub in range(subs):
                landed(piece(block, 1 - y, sub), side_recv.at[block * subs + sub])


def gather_over_samp(x, samp_count):
    rows, cols = grid_place(samp_count)
    subs = 4 if rows <= 4 and x.shape[0] % 4 == 0 else 1
    dma = pltpu.SemaphoreType.DMA
    line = dma((rows * subs,))
    return pl.pallas_call(
        functools.partial(gather_kernel, rows, cols, subs),
        out_shape=jax.ShapeDtypeStruct((samp_count,) + x.shape, x.dtype),
        in_specs=[VMEM_SPEC],
        out_specs=VMEM_SPEC,
        scratch_shapes=[line, line, line, line, dma((2 * rows * subs,)), line],
        compiler_params=pltpu.CompilerParams(
            collective_id=0, has_side_effects=True, vmem_limit_bytes=6 << 20),
        name="bias_gather",
    )(x)


def chunk_order(rows):
    order = []
    for k in range((rows + 1) // 2):
        order.append(rows - 1 - k)
        if k != rows - 1 - k:
            order.append(k)
    return order


def scatter_kernel(rows, cols, toks, subs, small, *refs):
    refs = list(refs)
    x_ref = refs.pop(0)
    small_ref = refs.pop(0) if small else None
    out_ref = refs.pop(0)
    small_out = refs.pop(0) if small else None
    (core_recv, side_buf, side_recv, total, line_buf, right_buf, left_buf,
     core_ss, core_rs, side_ss, side_rs, line_ss, right_rs, left_rs) = refs[:14]
    me = lax.axis_index("samp")
    z, y = me // cols, me % cols
    t = lax.axis_index("tok") if toks == 2 else 0
    samp_count = rows * cols
    if small:
        all_buf, all_ss, all_rs = refs[14:]
        flat = me * toks + t
        everyone = samp_count * toks
        barrier = pltpu.get_barrier_semaphore()
        peers = []
        for step in range(1, everyone):
            peer = lax.rem(flat + step, everyone)
            peers.append({"samp": peer // toks, "tok": peer % toks})
        for peer in peers:
            pl.semaphore_signal(barrier, 1, device_id=peer, device_id_type=MESH_ID)
        pl.semaphore_wait(barrier, everyone - 1)
        small_copies = [
            pltpu.make_async_remote_copy(
                src_ref=small_ref, dst_ref=all_buf.at[k], send_sem=all_ss.at[k],
                recv_sem=all_rs.at[k], device_id=peer, device_id_type=MESH_ID)
            for k, peer in enumerate(peers)]
    else:
        greet_line(rows, cols, z, y)
        small_copies = []

    order = chunk_order(rows)
    work = [(d, sub) for d in order for sub in range(subs)]
    span = out_ref.shape[0] // subs

    def cut(sub):
        return pl.ds(sub * span, span)

    def core_copy(index, sub):
        return pltpu.make_async_remote_copy(
            src_ref=x_ref.at[index, 1 - t, cut(sub)], dst_ref=core_recv.at[index, cut(sub)],
            send_sem=core_ss.at[index * subs + sub], recv_sem=core_rs.at[index * subs + sub],
            device_id={"tok": 1 - t}, device_id_type=MESH_ID)

    def send(src, dst, d, sub, send_sem, recv_sem, target):
        return pltpu.make_async_remote_copy(
            src_ref=src.at[d, cut(sub)], dst_ref=dst.at[d, cut(sub)],
            send_sem=send_sem.at[d * subs + sub], recv_sem=recv_sem.at[d * subs + sub],
            device_id=target, device_id_type=MESH_ID)

    def side_copy(d, sub):
        return send(side_buf, side_recv, d, sub, side_ss, side_rs, at_samp(z, 1 - y, cols))

    def right_copy(d, sub):
        return send(line_buf, right_buf, d, sub, line_ss, right_rs, at_samp(z + 1, y, cols))

    def left_copy(d, sub):
        return send(line_buf, left_buf, d, sub, line_ss, left_rs, at_samp(z - 1, y, cols))

    if toks == 2:
        for d, sub in work:
            if cols == 2:
                core_copy(d * cols + 1 - y, sub).start()
        for d, sub in work:
            core_copy(d * cols + y, sub).start()
    for copy in small_copies:
        copy.start()

    def local_sum(index, sub):
        value = x_ref[index, t, cut(sub)].astype(F32)
        if toks == 2:
            core_copy(index, sub).wait_recv()
            value = value + core_recv[index, cut(sub)].astype(F32)
        return value

    def side_send(d, sub):
        if toks == 2:
            side_buf[d, cut(sub)] = local_sum(d * cols + 1 - y, sub).astype(BF16)
            side_copy(d, sub).start()
        else:
            raw_side(d, sub).start()

    def raw_side(d, sub):
        return pltpu.make_async_remote_copy(
            src_ref=x_ref.at[d * cols + 1 - y, 0, cut(sub)], dst_ref=side_recv.at[d, cut(sub)],
            send_sem=side_ss.at[d * subs + sub], recv_sem=side_rs.at[d * subs + sub],
            device_id=at_samp(z, 1 - y, cols), device_id_type=MESH_ID)

    if cols == 2:
        for d, sub in work:
            side_send(d, sub)
    for d, sub in work:
        value = local_sum(d * cols + y, sub)
        if cols == 2:
            side_copy(d, sub).wait_recv()
            value = value + side_recv[d, cut(sub)].astype(F32)
        total[cut(sub)] = value

        @pl.when(z < d)
        def _():
            @pl.when(z > 0)
            def _():
                right_copy(d, sub).wait_recv()
                line_buf[d, cut(sub)] = (
                    total[cut(sub)] + right_buf[d, cut(sub)].astype(F32)).astype(BF16)

            @pl.when(z == 0)
            def _():
                line_buf[d, cut(sub)] = total[cut(sub)].astype(BF16)
            right_copy(d, sub).start()

        @pl.when(z > d)
        def _():
            @pl.when(z < rows - 1)
            def _():
                left_copy(d, sub).wait_recv()
                line_buf[d, cut(sub)] = (
                    total[cut(sub)] + left_buf[d, cut(sub)].astype(F32)).astype(BF16)

            @pl.when(z == rows - 1)
            def _():
                line_buf[d, cut(sub)] = total[cut(sub)].astype(BF16)
            left_copy(d, sub).start()

        @pl.when(z == d)
        def _():
            out_ref[cut(sub)] = total[cut(sub)]

    for sub in range(subs):
        @pl.when(z > 0)
        def _():
            right_copy(z, sub).wait_recv()
            out_ref[cut(sub)] += right_buf[z, cut(sub)].astype(F32)

        @pl.when(z < rows - 1)
        def _():
            left_copy(z, sub).wait_recv()
            out_ref[cut(sub)] += left_buf[z, cut(sub)].astype(F32)

    if small:
        whole = small_ref[...]
        for k, copy in enumerate(small_copies):
            copy.wait_recv()
            whole = whole + all_buf[k]
        small_out[...] = whole
    for copy in small_copies:
        copy.wait_send()
    for d, sub in work:
        pl.when(z < d)(lambda: right_copy(d, sub).wait_send())
        pl.when(z > d)(lambda: left_copy(d, sub).wait_send())
        if cols == 2:
            side_copy(d, sub).wait_send()
        if toks == 2:
            for c in range(cols):
                core_copy(d * cols + c, sub).wait_send()


def scatter_over_samp(x, collective_id, small=None):
    samp_count, toks = x.shape[:2]
    chunk = x.shape[2:]
    rows, cols = grid_place(samp_count)
    even = chunk[0] % 4 == 0 and (len(chunk) > 2 or chunk[0] % 64 == 0)
    subs = 4 if rows <= 4 and even else 1
    dma = pltpu.SemaphoreType.DMA
    line = pltpu.VMEM((rows,) + chunk, BF16)
    scratch = [
        pltpu.VMEM(((samp_count if toks == 2 else 1),) + chunk, BF16),
        line, line, pltpu.VMEM(chunk, F32), line, line, line,
        dma((samp_count * subs,)), dma((samp_count * subs,))] + [dma((rows * subs,))] * 5
    out_shape = [jax.ShapeDtypeStruct(chunk, F32)]
    operands = [x]
    if small is not None:
        everyone = samp_count * toks
        scratch += [pltpu.VMEM((everyone,) + small.shape, F32), dma((everyone,)), dma((everyone,))]
        out_shape.append(jax.ShapeDtypeStruct(small.shape, F32))
        operands.append(small)
    return pl.pallas_call(
        functools.partial(scatter_kernel, rows, cols, toks, subs, small is not None),
        out_shape=out_shape,
        in_specs=[VMEM_SPEC] * len(operands),
        out_specs=[VMEM_SPEC] * len(out_shape),
        scratch_shapes=scratch,
        compiler_params=pltpu.CompilerParams(
            collective_id=collective_id, has_side_effects=True,
            vmem_limit_bytes=(24 if toks == 2 else 12) << 20),
        name=f"scatter{collective_id}",
    )(*operands)


def dot(a, b, ca, cb):
    return lax.dot_general(a, b, (((ca,), (cb,)), ((), ())), preferred_element_type=F32)


def attention_kernel(scale, tiled, bias_ref, chain_j_ref, chain_i_ref, q_ref, u_ref,
                     k_own_ref, k_far_ref, v_own_ref, v_far_ref,
                     mixed_ref, dq_ref, dk_own_ref, dk_far_ref, dv_own_ref, dv_far_ref, ds_ref,
                     k_buf, v_buf, dk_buf, dv_buf):
    pairs, size, lanes = q_ref.shape
    half = k_own_ref.shape[0]
    keys = k_buf.shape[0]
    t = lax.axis_index("tok")
    if keys == half:
        own = far = pl.ds(0, half)
    else:
        own, far = pl.ds(t * half, half), pl.ds((1 - t) * half, half)
    k_buf[far] = k_far_ref[...]
    v_buf[far] = v_far_ref[...]
    k_buf[own] = k_own_ref[...]
    v_buf[own] = v_own_ref[...]
    first_head = lax.broadcasted_iota(jnp.int32, (size, lanes), 1) < lanes // 2

    def spread(packed):
        zero = jnp.zeros_like(packed)
        return jnp.concatenate(
            [jnp.where(first_head, packed, zero), jnp.where(first_head, zero, packed)], axis=0)

    def pick(wide):
        return jnp.where(first_head, wide[:size], wide[size:])

    for g in range(pairs):
        span = slice(2 * size * g, 2 * size * (g + 1))
        query = spread(q_ref[g])
        upstream = spread(u_ref[g])
        key = k_buf[:, span]
        value = v_buf[:, span]
        bias = (bias_ref[:, g] if tiled else bias_ref[g]).astype(F32).reshape(keys, lanes)
        reward = jnp.where(chain_j_ref[...] == chain_i_ref[...], CHAIN_REWARD, 0.0)
        scores = dot(key, query, 1, 0) * scale + (bias + reward)
        peak = jnp.max(scores, axis=0, keepdims=True)
        terms = jnp.exp(scores - peak)
        probs = terms * (1.0 / jnp.sum(terms, axis=0, keepdims=True))
        low = probs.astype(BF16)
        prob_grad = dot(value, upstream, 1, 0)
        middle = jnp.sum(probs * prob_grad, axis=0, keepdims=True)
        score_low = (probs * (prob_grad - middle)).astype(BF16)
        mixed_ref[g] = pick(dot(value, low, 0, 0)).astype(BF16)
        dq_ref[g] = (pick(dot(key, score_low, 0, 0)) * scale).astype(BF16)
        dk_buf[:, span] = (dot(score_low, query, 1, 1) * scale).astype(BF16)
        dv_buf[:, span] = dot(low, upstream, 1, 1).astype(BF16)
        if tiled:
            ds_ref[:, g] = score_low.reshape(ds_ref.shape[0], ds_ref.shape[2], lanes)
        else:
            ds_ref[g] = score_low
    dk_own_ref[...] = dk_buf[own]
    dk_far_ref[...] = dk_buf[far]
    dv_own_ref[...] = dv_buf[own]
    dv_far_ref[...] = dv_buf[far]


def attention(scale, bias, chain_j, chain_i, q, u, k_own, k_far, v_own, v_far):
    pairs, size, lanes = q.shape
    half, width = k_own.shape
    keys = chain_j.shape[0]
    samp_count, _, part, _ = bias.shape
    tiled = part % 16 == 0
    if not tiled:
        bias = bias.transpose(1, 0, 2, 3).reshape(pairs, keys, lanes)
    packed = jax.ShapeDtypeStruct((pairs, size, lanes), BF16)
    flat = jax.ShapeDtypeStruct((half, width), BF16)
    *grads, ds = pl.pallas_call(
        functools.partial(attention_kernel, scale, tiled),
        in_specs=[VMEM_SPEC] * 9,
        out_specs=[VMEM_SPEC] * 7,
        out_shape=[packed] * 2 + [flat] * 4 + [jax.ShapeDtypeStruct(bias.shape, BF16)],
        scratch_shapes=[pltpu.VMEM((keys, width), BF16)] * 4,
        compiler_params=pltpu.CompilerParams(vmem_limit_bytes=16 << 20),
        name="attention_backward",
    )(bias, chain_j, chain_i, q, u, k_own, k_far, v_own, v_far)
    if not tiled:
        ds = ds.reshape(pairs, samp_count, part, lanes).transpose(1, 0, 2, 3)
    return (*grads, ds)


def per_device(acts, out_grad, pair, chain_of_token, w_query, w_key, w_value, w_out, w_pair):
    samples, row_count, width = acts.shape
    assert samples == 1
    heads = w_pair.shape[1]
    size = width // heads
    pairs = heads // 2
    toks = lax.axis_size("tok")
    samp_count = lax.axis_size("samp")
    keys = row_count * toks
    part = pair.shape[1]
    lanes = 2 * row_count
    scale = 1.0 / math.sqrt(size)
    t = lax.axis_index("tok")

    tile = jnp.einsum("ijc,cpa->pjai", pair, w_pair.reshape(-1, pairs, 2),
                      preferred_element_type=F32).astype(BF16).reshape(pairs, part, lanes)
    bias = gather_over_samp(tile, samp_count)

    rows = acts[0]
    grad_rows = out_grad[0]
    k_own = jnp.dot(rows, w_key, preferred_element_type=F32).astype(BF16)
    v_own = jnp.dot(rows, w_value, preferred_element_type=F32).astype(BF16)
    swap = [(a, (a + 1) % toks) for a in range(toks)]
    k_far = lax.ppermute(k_own, "tok", swap)
    v_far = lax.ppermute(v_own, "tok", swap)

    def packed(flat_t):
        return flat_t.reshape(pairs, 2, size, row_count).transpose(0, 2, 1, 3).reshape(
            pairs, size, lanes)

    def unpacked(p):
        return p.reshape(pairs, size, 2, row_count).transpose(0, 2, 1, 3).reshape(width, row_count)

    q = packed(dot(w_query, rows, 0, 1).astype(BF16))
    u = packed(dot(w_out, grad_rows, 1, 1).astype(BF16))
    own_chain = lax.dynamic_slice_in_dim(chain_of_token, t * row_count, row_count, 0)
    chain_i = jnp.concatenate([own_chain, own_chain])[None, :]
    mixed, dq, dk_own, dk_far, dv_own, dv_far, ds = attention(
        scale, bias, chain_of_token[:, None], chain_i, q, u, k_own, k_far, v_own, v_far)

    bias_grad = scatter_over_samp(
        ds.reshape(samp_count, 1, pairs, part, lanes), 1)[0].astype(BF16)

    def summed(mine, sent):
        if toks == 1:
            return mine
        return (mine.astype(F32) + lax.ppermute(sent, "tok", swap).astype(F32)).astype(BF16)

    dk = summed(dk_own, dk_far)
    dv = summed(dv_own, dv_far)
    dq_t = unpacked(dq)
    mixed_t = unpacked(mixed)
    act_grad = dot(dq_t, w_query, 0, 1) + dot(dk, w_key, 1, 1) + dot(dv, w_value, 1, 1)
    act_grad = act_grad.astype(BF16)[None]
    stacked = jnp.concatenate([
        dot(rows, dq_t, 0, 1).astype(BF16),
        dot(rows, dk, 0, 0).astype(BF16),
        dot(rows, dv, 0, 0).astype(BF16),
        dot(mixed_t, grad_rows, 1, 0).astype(BF16)], 0)
    grouped = stacked.reshape(samp_count, toks, -1, width)
    by_head = bias_grad.reshape(pairs, part, 2, row_count).transpose(3, 1, 0, 2)
    by_head = lax.optimization_barrier(by_head.reshape(row_count * part, heads))
    pair_grad = dot(by_head, w_pair, 1, 1).reshape(pair.shape)
    pair_term = dot(by_head, pair.reshape(row_count * part, -1), 0, 0)
    weight_grads, pair_weight = scatter_over_samp(grouped, 2, pair_term)
    return act_grad, pair_grad, weight_grads, pair_weight.T


def solution(mesh):
    in_specs = (
        P(("job", "samp"), "tok", None),
        P(("job", "samp"), "tok", None),
        P(("job", "tok"), "samp", None),
        P("job"),
        P(),
        P(),
        P(),
        P(),
        P(),
    )
    out_specs = (
        P(("job", "samp"), "tok", None),
        P(("job", "tok"), "samp", None),
        P(("job", "samp", "tok"), None),
        P("job", None),
    )
    return jax.shard_map(
        per_device, mesh=mesh, in_specs=in_specs, out_specs=out_specs, check_vma=False
    )
```
